32 devices in a mesh: space: 16 (over z, y, core), samp: 2 (over x).
Axes of the slice: x: 2, y: 2, z: 4, core: 2. Of those that a mesh axis runs over, the one named last changes fastest.
Arguments:
- snapshots: float32 [4, 512, 32768], P(None, 'samp', 'space'), may hold values from -24 to 24
- space_basis: float32 [256, 32768], P('samp', 'space'), may hold values from -0.03314563 to 0.03314563
- sample_basis: float32 [512, 64], P('samp'), may hold values from -0.26516504 to 0.26516504
Outputs:
- deflated: float32 [4, 512, 32768], P(None, 'samp', 'space')
The draws below stay inside these ranges and needn't reach their ends.
All inputs are finite; a program needn't handle non-finite values.
Results may differ from the reference program's by a relative error of at most 0.000078.
Values sent between devices are 32-bit elements; how exact they have to be, the bound alone decides.
No kernel may reach another device: no remote copies, remote signals or barrier semaphores. Data moves between devices by JAX's collectives and lax.ppermute only.
A program may use at most 64 MiB of HBM per device.

```python
import math
import jax
import jax.numpy as jnp
from jax import lax

SAMPLES = 512
RANK_SPACE = 256
RANK_SAMP = 64
SNAPS = 4
SPACE = 32768


def common_factors(key):
    base_key = jax.random.fold_in(key, 101)
    key_space, key_sample, key_amplitude, key_noise = jax.random.split(base_key, 4)
    space_factor = jax.random.truncated_normal(key_space, -6.0, 6.0, (RANK_SPACE, SPACE), jnp.float32) / math.sqrt(SPACE)
    sample_factor = jax.random.truncated_normal(key_sample, -6.0, 6.0, (SAMPLES, RANK_SAMP), jnp.float32) / math.sqrt(SAMPLES)
    amplitudes = jax.random.normal(key_amplitude, (SNAPS, RANK_SPACE, RANK_SAMP), jnp.float32)
    amplitudes = amplitudes * (0.8 * math.sqrt(SPACE * SAMPLES / (RANK_SPACE * RANK_SAMP)))
    return (space_factor, sample_factor, amplitudes, key_noise)


def draw_space_basis(key, part):
    return common_factors(key)[0]


def draw_sample_basis(key, part):
    return common_factors(key)[1]


def draw_snapshots(key, part):
    space_factor, sample_factor, amplitudes, key_noise = common_factors(key)
    highest = lax.Precision.HIGHEST
    spread = jnp.einsum('trq,sq->trs', amplitudes, sample_factor, precision=highest)
    signal = jnp.einsum('trs,rm->tsm', spread, space_factor, precision=highest)
    independent = jax.random.normal(key_noise, (SNAPS, SAMPLES, SPACE), jnp.float32)
    return jnp.clip(signal + independent, -24.0, 24.0)


def setup_inputs(seed: int = 0) -> dict:
    key_of = jax.random.split(jax.random.key(seed), 4)
    return {
        "snapshots": draw_snapshots(jax.random.fold_in(key_of[3], 71), 0),
        "space_basis": draw_space_basis(jax.random.fold_in(key_of[3], 71), 0),
        "sample_basis": draw_sample_basis(jax.random.fold_in(key_of[3], 71), 0),
    }


def reference(snapshots, space_basis, sample_basis):
    highest = lax.Precision.HIGHEST
    contracted = jnp.einsum("rm,tsm->rts", space_basis, snapshots, precision=highest)
    core_full = jnp.einsum("rts,sq->rtq", contracted, sample_basis, precision=highest)
    spread = jnp.einsum("rtq,sq->rts", core_full, sample_basis, precision=highest)
    removed = jnp.einsum("rts,rm->tsm", spread, space_basis, precision=highest)
    return snapshots - removed
```

```python
import jax
import jax.numpy as jnp
from jax import lax
from jax.sharding import PartitionSpec as P


def swap(value, axis, size, bit):
    return lax.ppermute(value, axis, [(i, i ^ bit) for i in range(size)])


def bits(size, start=1):
    while start < size:
        yield start
        start *= 2


def solution(mesh):
    space, samp = mesh.shape["space"], mesh.shape["samp"]
    highest = lax.Precision.HIGHEST

    def dot(a, b, dims):
        return lax.dot_general(a, b, (dims, ((), ())), precision=highest, preferred_element_type=jnp.float32)

    def over_space(part):
        core = lax.axis_index("space") % 2
        half = part.shape[-2] // 2
        low, high = part[..., :half, :], part[..., half:, :]
        mine = jnp.where(core == 0, low, high)
        total = mine + swap(jnp.where(core == 0, high, low), "space", space, 1)
        for bit in bits(space, 2):
            total = total + swap(total, "space", space, bit)
        return total

    def shards(snapshots, space_basis, sample_basis):
        snaps, samples, columns = snapshots.shape
        rank = sample_basis.shape[1]
        bases = [space_basis]
        for d in range(1, samp):
            bases.append(swap(space_basis, "samp", samp, d))
        mixed = lax.dot_general(
            sample_basis, snapshots, (((0,), (1,)), ((), ())), precision=highest,
            preferred_element_type=jnp.float32)
        mixed = mixed.transpose(1, 0, 2).reshape(snaps * rank, columns)
        own = over_space(dot(mixed, space_basis, ((1,), (1,))))
        rest = over_space(jnp.stack([dot(mixed, b, ((1,), (1,))) for b in bases[1:]]))
        core = jnp.concatenate([own[None], rest])
        for bit in bits(samp):
            got = swap(core, "samp", samp, bit)
            core = core + jnp.stack([got[d ^ bit] for d in range(samp)])
        other = swap(core, "space", space, 1)
        first = lax.axis_index("space") % 2 == 0
        core = jnp.concatenate([jnp.where(first, core, other), jnp.where(first, other, core)], axis=1)
        weight = sum(dot(core[d], bases[d], ((1,), (0,))) for d in range(samp))
        weight = weight.reshape(snaps, rank, columns)
        removed = lax.dot_general(
            sample_basis, weight, (((1,), (1,)), ((), ())), precision=highest,
            preferred_element_type=jnp.float32)
        return snapshots - removed.transpose(1, 0, 2)

    return jax.shard_map(
        shards,
        mesh=mesh,
        in_specs=(P(None, "samp", "space"), P("samp", "space"), P("samp", None)),
        out_specs=P(None, "samp", "space"),
        check_vma=False,
    )
```

```python
import functools

import jax
import jax.numpy as jnp
from jax import lax
from jax.experimental import pallas as pl
from jax.experimental.pallas import tpu as pltpu
from jax.sharding import PartitionSpec as P

MIB = 1 << 20


def swap(value, axis, size, bit):
    return lax.ppermute(value, axis, [(i, i ^ bit) for i in range(size)])


def bits(size, start=1):
    while start < size:
        yield start
        start *= 2


def tile_of(columns):
    for tile in (512, 256, 128):
        if columns % tile == 0:
            return tile
    return columns


def split(value):
    high = value.astype(jnp.bfloat16)
    return high, (value - high.astype(jnp.float32)).astype(jnp.bfloat16)


def mul(a, b):
    return lax.dot_general(a, b, (((1,), (0,)), ((), ())), preferred_element_type=jnp.float32)


def mul_t(a, b):
    return lax.dot_general(a, b, (((1,), (1,)), ((), ())), preferred_element_type=jnp.float32)


def rows_times(y_high, y_low, b):
    rank = b.shape[0]
    high, low = split(b)
    both = mul_t(y_high, jnp.concatenate([high, low], axis=0))
    return both[:, :rank] + both[:, rank:] + mul_t(y_low, high), high, low


def first_kernel(tile, x_hbm, s_ref, b_hbm, x_ref, y_ref, bs_ref, part_ref, b_ref, sems, b_sem):
    snaps, samples, columns = x_ref.shape
    rank = s_ref.shape[0]
    steps = columns // tile
    copies = []
    for j in range(steps):
        cols = pl.ds(j * tile, tile)
        copies.append(pltpu.make_async_copy(x_hbm.at[:, :, cols], x_ref.at[:, :, cols], sems.at[j]))
    b_copy = pltpu.make_async_copy(b_hbm, b_ref, b_sem)
    copies[0].start()
    b_copy.start()
    for copy in copies[1:]:
        copy.start()
    s_high, s_low = split(s_ref[...])
    s_both = jnp.concatenate([s_high, s_low], axis=0)
    for j in range(steps):
        cols = pl.ds(j * tile, tile)
        copies[j].wait()
        if j == 0:
            b_copy.wait()
        for t in range(snaps):
            x_high, x_low = split(x_ref[t, :, cols])
            both = mul(s_both, x_high)
            y = both[:rank] + both[rank:] + mul(s_high, x_low)
            y_high, y_low = split(y)
            y_ref[0, t * rank:(t + 1) * rank, cols] = y_high
            y_ref[1, t * rank:(t + 1) * rank, cols] = y_low
        total, high, low = rows_times(y_ref[0, :, cols], y_ref[1, :, cols], b_ref[:, cols])
        bs_ref[0, :, cols] = high
        bs_ref[1, :, cols] = low
        if j == 0:
            part_ref[...] = total
        else:
            part_ref[...] += total


def second_kernel(tile, parts, *refs):
    b_refs, (y_ref, _), outs = refs[:parts], refs[parts:parts + 2], refs[parts + 2:]
    part_ref, bs_refs = outs[0], outs[1:]
    for d in range(parts):
        for j in range(y_ref.shape[2] // tile):
            cols = pl.ds(j * tile, tile)
            total, high, low = rows_times(y_ref[0, :, cols], y_ref[1, :, cols], b_refs[d][:, cols])
            bs_refs[d][0, :, cols] = high
            bs_refs[d][1, :, cols] = low
            if j == 0:
                part_ref[d] = total
            else:
                part_ref[d] += total


def last_kernel(tile, parts, *refs):
    core_ref, s_ref, x_ref = refs[:3]
    bs_refs, out_hbm, out_ref, sems = refs[3:3 + parts], refs[3 + parts], refs[4 + parts], refs[5 + parts]
    snaps, samples, columns = x_ref.shape
    rank = s_ref.shape[0]
    s_high, s_low = split(s_ref[...].T)
    s_all = jnp.concatenate([s_high, s_low, s_high], axis=1)
    c_high, c_low = split(jnp.concatenate([core_ref[d] for d in range(parts)], axis=1))
    c_both = jnp.concatenate([c_high, c_low], axis=0)
    wide = c_high.shape[0]
    copies = []
    for j in range(columns // tile):
        cols = pl.ds(j * tile, tile)
        b_high = jnp.concatenate([b[0, :, cols] for b in bs_refs], axis=0)
        b_low = jnp.concatenate([b[1, :, cols] for b in bs_refs], axis=0)
        both = mul(c_both, b_high)
        weight = both[:wide] + both[wide:] + mul(c_high, b_low)
        w_high, w_low = split(weight)
        for t in range(snaps):
            high, low = w_high[t * rank:(t + 1) * rank], w_low[t * rank:(t + 1) * rank]
            removed = mul(s_all, jnp.concatenate([high, high, low], axis=0))
            out_ref[t, :, cols] = x_ref[t, :, cols] - removed
        copies.append(pltpu.make_async_copy(out_ref.at[:, :, cols], out_hbm.at[:, :, cols], sems.at[j]))
        copies[-1].start()
    for copy in copies:
        copy.wait()


VMEM = pl.BlockSpec(memory_space=pltpu.VMEM)
ANY = pl.BlockSpec(memory_space=pl.ANY)
HBM = pl.BlockSpec(memory_space=pltpu.HBM)


def on_chip(shape, dtype):
    return pltpu.VMEM(shape, dtype)


def solution(mesh):
    space, samp = mesh.shape["space"], mesh.shape["samp"]

    def over_space(part):
        core = lax.axis_index("space") % 2
        half = part.shape[-2] // 2
        low, high = part[..., :half, :], part[..., half:, :]
        mine = jnp.where(core == 0, low, high)
        total = mine + swap(jnp.where(core == 0, high, low), "space", space, 1)
        for bit in bits(space, 2):
            total = total + swap(total, "space", space, bit)
        return total

    def shards(snapshots, space_basis, sample_basis):
        snaps, samples, columns = snapshots.shape
        rank = sample_basis.shape[1]
        basis_rows = space_basis.shape[0]
        wide = snaps * rank
        tile = tile_of(columns)
        steps = columns // tile
        others = [swap(space_basis, "samp", samp, d) for d in range(1, samp)]
        mixer = sample_basis.T
        flops = 6 * wide * samples * columns
        x_chip, mixed, own_split, own = pl.pallas_call(
            functools.partial(first_kernel, tile),
            out_shape=(
                on_chip(snapshots.shape, jnp.float32),
                on_chip((2, wide, columns), jnp.bfloat16),
                on_chip((2, basis_rows, columns), jnp.bfloat16),
                on_chip((wide, basis_rows), jnp.float32),
            ),
            in_specs=[HBM, VMEM, HBM],
            out_specs=(VMEM,) * 4,
            scratch_shapes=[
                pltpu.VMEM((basis_rows, columns), jnp.float32),
                pltpu.SemaphoreType.DMA((steps,)),
                pltpu.SemaphoreType.DMA,
            ],
            compiler_params=pltpu.CompilerParams(vmem_limit_bytes=48 * MIB),
            cost_estimate=pl.CostEstimate(flops=flops, bytes_accessed=snapshots.size * 4, transcendentals=0),
            name="first",
        )(snapshots, mixer, space_basis)
        own = over_space(own)
        rest, *rest_splits = pl.pallas_call(
            functools.partial(second_kernel, tile, samp - 1),
            out_shape=(
                on_chip((samp - 1, wide, basis_rows), jnp.float32),
                *[on_chip((2, basis_rows, columns), jnp.bfloat16) for _ in others],
            ),
            in_specs=[VMEM] * (len(others) + 1) + [ANY],
            out_specs=(VMEM,) * samp,
            compiler_params=pltpu.CompilerParams(vmem_limit_bytes=16 * MIB),
            cost_estimate=pl.CostEstimate(
                flops=6 * wide * basis_rows * columns * (samp - 1), bytes_accessed=0, transcendentals=0),
            name="second",
        )(*others, mixed, own)
        rest = over_space(rest)
        core = jnp.concatenate([own[None], rest])
        for bit in bits(samp):
            got = swap(core, "samp", samp, bit)
            core = core + jnp.stack([got[d ^ bit] for d in range(samp)])
        other = swap(core, "space", space, 1)
        first = lax.axis_index("space") % 2 == 0
        core = jnp.concatenate([jnp.where(first, core, other), jnp.where(first, other, core)], axis=1)
        return pl.pallas_call(
            functools.partial(last_kernel, tile, samp),
            out_shape=jax.ShapeDtypeStruct(snapshots.shape, jnp.float32),
            in_specs=[VMEM] * (3 + samp),
            out_specs=ANY,
            scratch_shapes=[
                pltpu.VMEM(snapshots.shape, jnp.float32),
                pltpu.SemaphoreType.DMA((steps,)),
            ],
            compiler_params=pltpu.CompilerParams(vmem_limit_bytes=20 * MIB),
            cost_estimate=pl.CostEstimate(flops=2 * flops, bytes_accessed=snapshots.size * 4, transcendentals=0),
            name="last",
        )(core, mixer, x_chip, own_split, *rest_splits)

    return jax.shard_map(
        shards,
        mesh=mesh,
        in_specs=(P(None, "samp", "space"), P("samp", "space"), P("samp", None)),
        out_specs=P(None, "samp", "space"),
        check_vma=False,
    )
```

```python
import functools

import jax
import jax.numpy as jnp
from jax import lax
from jax.experimental import pallas as pl
from jax.experimental.pallas import tpu as pltpu
from jax.sharding import PartitionSpec as P


MIB = 1 << 20


def swap(value, axis, size, bit):
    return lax.ppermute(value, axis, [(i, i ^ bit) for i in range(size)])


def bits(size, start=1):
    while start < size:
        yield start
        start *= 2


def swap_both(value, space, samp, bit, other):
    perm = [(i * samp + j, (i ^ bit) * samp + (j ^ other)) for i in range(space) for j in range(samp)]
    return lax.ppermute(value, ("space", "samp"), perm)


def tile_of(columns):
    for tile in (512, 256, 128):
        if columns % tile == 0:
            return tile
    return columns


def split(value):
    high = value.astype(jnp.bfloat16)
    return high, (value - high.astype(jnp.float32)).astype(jnp.bfloat16)


def mul(a, b):
    return lax.dot_general(a, b, (((1,), (0,)), ((), ())), preferred_element_type=jnp.float32)


def mul_t(a, b):
    return lax.dot_general(a, b, (((1,), (1,)), ((), ())), preferred_element_type=jnp.float32)


def rows_times(y_high, y_low, b):
    rank = b.shape[0]
    high, low = split(b)
    both = mul_t(y_high, jnp.concatenate([high, low], axis=0))
    return both[:, :rank] + both[:, rank:] + mul_t(y_low, high), high, low


def first_kernel(tile, x_hbm, s_ref, b_hbm, x_ref, y_ref, bs_ref, part_ref, b_ref, sems, b_sem):
    snaps, _, columns = x_ref.shape
    rank = s_ref.shape[0]
    steps = columns // tile
    copies = []
    for j in range(steps):
        cols = pl.ds(j * tile, tile)
        copies.append(pltpu.make_async_copy(x_hbm.at[:, :, cols], x_ref.at[:, :, cols], sems.at[j]))
    b_copy = pltpu.make_async_copy(b_hbm, b_ref, b_sem)
    copies[0].start()
    b_copy.start()
    for copy in copies[1:]:
        copy.start()
    s_high, s_low = split(s_ref[...])
    s_both = jnp.concatenate([s_high, s_low], axis=0)
    for j in range(steps):
        cols = pl.ds(j * tile, tile)
        copies[j].wait()
        if j == 0:
            b_copy.wait()
        for t in range(snaps):
            x_high, x_low = split(x_ref[t, :, cols])
            both = mul(s_both, x_high)
            y = both[:rank] + both[rank:] + mul(s_high, x_low)
            y_high, y_low = split(y)
            y_ref[0, t * rank:(t + 1) * rank, cols] = y_high
            y_ref[1, t * rank:(t + 1) * rank, cols] = y_low
        total, high, low = rows_times(y_ref[0, :, cols], y_ref[1, :, cols], b_ref[:, cols])
        bs_ref[0, :, cols] = high
        bs_ref[1, :, cols] = low
        if j == 0:
            part_ref[...] = total
        else:
            part_ref[...] += total


def second_kernel(tile, parts, *refs):
    b_refs, (y_ref, _), outs = refs[:parts], refs[parts:parts + 2], refs[parts + 2:]
    part_ref, bs_refs = outs[0], outs[1:]
    for d in range(parts):
        for j in range(y_ref.shape[2] // tile):
            cols = pl.ds(j * tile, tile)
            total, high, low = rows_times(y_ref[0, :, cols], y_ref[1, :, cols], b_refs[d][:, cols])
            bs_refs[d][0, :, cols] = high
            bs_refs[d][1, :, cols] = low
            if j == 0:
                part_ref[d] = total
            else:
                part_ref[d] += total


def last_kernel(tile, parts, *refs):
    core_ref, s_ref, x_ref = refs[:3]
    bs_refs, out_hbm, out_ref, sems = refs[3:3 + parts], refs[3 + parts], refs[4 + parts], refs[5 + parts]
    snaps, _, columns = x_ref.shape
    rank = s_ref.shape[0]
    s_high, s_low = split(s_ref[...].T)
    s_all = jnp.concatenate([s_high, s_low, s_high], axis=1)
    c_high, c_low = split(jnp.concatenate([core_ref[d] for d in range(parts)], axis=1))
    c_both = jnp.concatenate([c_high, c_low], axis=0)
    wide = c_high.shape[0]
    copies = []
    for j in range(columns // tile):
        cols = pl.ds(j * tile, tile)
        b_high = jnp.concatenate([b[0, :, cols] for b in bs_refs], axis=0)
        b_low = jnp.concatenate([b[1, :, cols] for b in bs_refs], axis=0)
        both = mul(c_both, b_high)
        weight = both[:wide] + both[wide:] + mul(c_high, b_low)
        w_high, w_low = split(weight)
        for t in range(snaps):
            high, low = w_high[t * rank:(t + 1) * rank], w_low[t * rank:(t + 1) * rank]
            removed = mul(s_all, jnp.concatenate([high, high, low], axis=0))
            out_ref[t, :, cols] = x_ref[t, :, cols] - removed
        copies.append(pltpu.make_async_copy(out_ref.at[:, :, cols], out_hbm.at[:, :, cols], sems.at[j]))
        copies[-1].start()
    for copy in copies:
        copy.wait()


VMEM = pl.BlockSpec(memory_space=pltpu.VMEM)
ANY = pl.BlockSpec(memory_space=pl.ANY)
HBM = pl.BlockSpec(memory_space=pltpu.HBM)


def on_chip(shape, dtype):
    return pltpu.VMEM(shape, dtype)


def solution(mesh):
    space, samp = mesh.shape["space"], mesh.shape["samp"]

    left = list(bits(space, 2))
    groups = []
    while len(left) > 1:
        groups.append((left[-1], left[-2] | left[-1], left[-2]))
        left = left[:-2]

    def halved(part):
        core = lax.axis_index("space") % 2
        half = part.shape[-2] // 2
        low, high = part[..., :half, :], part[..., half:, :]
        mine = jnp.where(core == 0, low, high)
        return mine + swap(jnp.where(core == 0, high, low), "space", space, 1)

    def over_groups(part):
        for group in groups:
            got = [swap(part, "space", space, bit) for bit in group]
            part = part + got[0] + got[1] + got[2]
        return part

    def over_rest(own, rest):
        done = [own] + [rest[d] for d in range(samp - 1)]
        for bit in bits(samp):
            if bit == 1:
                got_own = swap(own, "samp", samp, bit)
                far = [swap_both(rest, space, samp, b, bit) for b in left]
                got_rest = swap(rest, "samp", samp, bit)
                near = [swap(rest, "space", space, b) for b in left]
                got = [got_own]
                for d in range(1, samp):
                    value = got_rest[d - 1]
                    for f in far:
                        value = value + f[d - 1]
                    got.append(value)
                for n in near:
                    done = [done[0]] + [done[d] + n[d - 1] for d in range(1, samp)]
            else:
                got = swap(jnp.stack(done), "samp", samp, bit)
            done = [done[d] + got[d ^ bit] for d in range(samp)]
        return jnp.stack(done)

    def shards(snapshots, space_basis, sample_basis):
        snaps, samples, columns = snapshots.shape
        rank = sample_basis.shape[1]
        basis_rows = space_basis.shape[0]
        wide = snaps * rank
        tile = tile_of(columns)
        steps = columns // tile
        others = [swap(space_basis, "samp", samp, d) for d in range(1, samp)]
        mixer = sample_basis.T
        flops = 6 * wide * samples * columns
        x_chip, mixed, own_split, own = pl.pallas_call(
            functools.partial(first_kernel, tile),
            out_shape=(
                on_chip(snapshots.shape, jnp.float32),
                on_chip((2, wide, columns), jnp.bfloat16),
                on_chip((2, basis_rows, columns), jnp.bfloat16),
                on_chip((wide, basis_rows), jnp.float32),
            ),
            in_specs=[HBM, VMEM, HBM],
            out_specs=(VMEM,) * 4,
            scratch_shapes=[
                pltpu.VMEM((basis_rows, columns), jnp.float32),
                pltpu.SemaphoreType.DMA((steps,)),
                pltpu.SemaphoreType.DMA,
            ],
            compiler_params=pltpu.CompilerParams(vmem_limit_bytes=48 * MIB),
            cost_estimate=pl.CostEstimate(flops=flops, bytes_accessed=snapshots.size * 4, transcendentals=0),
            name="first",
        )(snapshots, mixer, space_basis)
        own = over_groups(halved(own))
        for bit in left:
            own = own + swap(own, "space", space, bit)
        rest, *rest_splits = pl.pallas_call(
            functools.partial(second_kernel, tile, samp - 1),
            out_shape=(
                on_chip((samp - 1, wide, basis_rows), jnp.float32),
                *[on_chip((2, basis_rows, columns), jnp.bfloat16) for _ in others],
            ),
            in_specs=[VMEM] * (len(others) + 1) + [ANY],
            out_specs=(VMEM,) * samp,
            compiler_params=pltpu.CompilerParams(vmem_limit_bytes=16 * MIB),
            cost_estimate=pl.CostEstimate(
                flops=6 * wide * basis_rows * columns * (samp - 1), bytes_accessed=0, transcendentals=0),
            name="second",
        )(*others, mixed, own)
        core = over_rest(own, over_groups(halved(rest)))
        other = swap(core, "space", space, 1)
        first = lax.axis_index("space") % 2 == 0
        core = jnp.concatenate([jnp.where(first, core, other), jnp.where(first, other, core)], axis=1)
        return pl.pallas_call(
            functools.partial(last_kernel, tile, samp),
            out_shape=jax.ShapeDtypeStruct(snapshots.shape, jnp.float32),
            in_specs=[VMEM] * (3 + samp),
            out_specs=ANY,
            scratch_shapes=[
                pltpu.VMEM(snapshots.shape, jnp.float32),
                pltpu.SemaphoreType.DMA((steps,)),
            ],
            compiler_params=pltpu.CompilerParams(vmem_limit_bytes=20 * MIB),
            cost_estimate=pl.CostEstimate(flops=2 * flops, bytes_accessed=snapshots.size * 4, transcendentals=0),
            name="last",
        )(core, mixer, x_chip, own_split, *rest_splits)

    return jax.shard_map(
        shards,
        mesh=mesh,
        in_specs=(P(None, "samp", "space"), P("samp", "space"), P("samp", None)),
        out_specs=P(None, "samp", "space"),
        check_vma=False,
    )
```

```python
import functools

import jax
import jax.numpy as jnp
from jax import lax
from jax.experimental import pallas as pl
from jax.experimental.pallas import tpu as pltpu
from jax.sharding import PartitionSpec as P


MIB = 1 << 20
AHEAD = 2


def swap(value, axis, size, bit):
    return lax.ppermute(value, axis, [(i, i ^ bit) for i in range(size)])


def bits(size, start=1):
    while start < size:
        yield start
        start *= 2


def swap_both(value, space, samp, bit, other):
    perm = [(i * samp + j, (i ^ bit) * samp + (j ^ other)) for i in range(space) for j in range(samp)]
    return lax.ppermute(value, ("space", "samp"), perm)


def tile_of(columns, most=512):
    for tile in (512, 256, 128):
        if tile <= most and columns % tile == 0:
            return tile
    return columns


def split(value):
    high = value.astype(jnp.bfloat16)
    return high, (value - high.astype(jnp.float32)).astype(jnp.bfloat16)


def mul(a, b):
    return lax.dot_general(a, b, (((1,), (0,)), ((), ())), preferred_element_type=jnp.float32)


def mul_t(a, b):
    return lax.dot_general(a, b, (((1,), (1,)), ((), ())), preferred_element_type=jnp.float32)


def rows_times(y_high, y_low, b):
    rank = b.shape[0]
    high, low = split(b)
    both = mul_t(y_high, jnp.concatenate([high, low], axis=0))
    return both[:, :rank] + both[:, rank:] + mul_t(y_low, high), high, low


def first_kernel(tile, x_hbm, s_ref, b_hbm, x_ref, y_ref, bs_ref, part_ref, spread_ref, b_ref, sems, b_sem):
    snaps, _, columns = x_ref.shape
    rank = s_ref.shape[0]
    steps = columns // tile
    copies = []
    for j in range(steps):
        cols = pl.ds(j * tile, tile)
        copies.append(pltpu.make_async_copy(x_hbm.at[:, :, cols], x_ref.at[:, :, cols], sems.at[j]))
    b_copy = pltpu.make_async_copy(b_hbm, b_ref, b_sem)
    copies[0].start()
    b_copy.start()
    for copy in copies[1:AHEAD]:
        copy.start()
    s_high, s_low = split(s_ref[...])
    s_both = jnp.concatenate([s_high, s_low], axis=0)
    t_high, t_low = split(s_ref[...].T)
    spread_ref[...] = jnp.concatenate([t_high, t_low, t_high], axis=1)
    for j in range(steps):
        cols = pl.ds(j * tile, tile)
        copies[j].wait()
        if j == 0:
            b_copy.wait()
        if j + AHEAD < steps:
            copies[j + AHEAD].start()
        for t in range(snaps):
            x_high, x_low = split(x_ref[t, :, cols])
            both = mul(s_both, x_high)
            y = both[:rank] + both[rank:] + mul(s_high, x_low)
            y_high, y_low = split(y)
            y_ref[0, t * rank:(t + 1) * rank, cols] = y_high
            y_ref[1, t * rank:(t + 1) * rank, cols] = y_low
        total, high, low = rows_times(y_ref[0, :, cols], y_ref[1, :, cols], b_ref[:, cols])
        bs_ref[0, :, cols] = high
        bs_ref[1, :, cols] = low
        if j == 0:
            part_ref[...] = total
        else:
            part_ref[...] += total


def second_kernel(tile, parts, *refs):
    b_refs, (y_ref, _), outs = refs[:parts], refs[parts:parts + 2], refs[parts + 2:]
    part_ref, bs_refs = outs[0], outs[1:]
    for d in range(parts):
        for j in range(y_ref.shape[2] // tile):
            cols = pl.ds(j * tile, tile)
            total, high, low = rows_times(y_ref[0, :, cols], y_ref[1, :, cols], b_refs[d][:, cols])
            bs_refs[d][0, :, cols] = high
            bs_refs[d][1, :, cols] = low
            if j == 0:
                part_ref[d] = total
            else:
                part_ref[d] += total


def last_kernel(tile, parts, mine, *refs):
    core_ref, s_ref, x_ref = refs[:3]
    bs_refs = refs[3:3 + parts]
    out_hbm, out_ref, w_ref, sems = refs[-4:]
    half, _, columns = out_ref.shape
    rank = s_ref.shape[1] // 3
    core = lax.axis_index("space") % 2
    start = half * (core if mine else 1 - core)
    c_high, c_low = split(jnp.concatenate([core_ref[d] for d in range(parts)], axis=1))
    c_both = jnp.concatenate([c_high, c_low], axis=0)
    wide = c_high.shape[0]
    steps = columns // tile

    def weigh(j):
        cols = pl.ds(j * tile, tile)
        b_high = jnp.concatenate([b[0, :, cols] for b in bs_refs], axis=0)
        b_low = jnp.concatenate([b[1, :, cols] for b in bs_refs], axis=0)
        both = mul(c_both, b_high)
        w_ref[0, :, cols], w_ref[1, :, cols] = split(both[:wide] + both[wide:] + mul(c_high, b_low))

    copies = []
    weigh(0)
    for j in range(steps):
        if j + 1 < steps:
            weigh(j + 1)
        cols = pl.ds(j * tile, tile)
        for t in range(half):
            high, low = w_ref[0, t * rank:(t + 1) * rank, cols], w_ref[1, t * rank:(t + 1) * rank, cols]
            removed = mul(s_ref[...], jnp.concatenate([high, high, low], axis=0))
            out_ref[t, :, cols] = x_ref[start + t, :, cols] - removed
        copies.append(pltpu.make_async_copy(
            out_ref.at[:, :, cols], out_hbm.at[pl.ds(start, half), :, cols], sems.at[j]))
        copies[-1].start()
    for copy in copies:
        copy.wait()


VMEM = pl.BlockSpec(memory_space=pltpu.VMEM)
ANY = pl.BlockSpec(memory_space=pl.ANY)
HBM = pl.BlockSpec(memory_space=pltpu.HBM)


def on_chip(shape, dtype):
    return pltpu.VMEM(shape, dtype)


def solution(mesh):
    space, samp = mesh.shape["space"], mesh.shape["samp"]

    left = list(bits(space, 2))
    groups = []
    while len(left) > 1:
        groups.append((left[-1], left[-2] | left[-1], left[-2]))
        left = left[:-2]

    def halved(part):
        core = lax.axis_index("space") % 2
        half = part.shape[-2] // 2
        low, high = part[..., :half, :], part[..., half:, :]
        mine = jnp.where(core == 0, low, high)
        return mine + swap(jnp.where(core == 0, high, low), "space", space, 1)

    def over_groups(part):
        for group in groups:
            got = [swap(part, "space", space, bit) for bit in group]
            part = part + got[0] + got[1] + got[2]
        return part

    def over_rest(own, rest):
        done = [own] + [rest[d] for d in range(samp - 1)]
        for bit in bits(samp):
            if bit == 1:
                got_own = swap(own, "samp", samp, bit)
                far = [swap_both(rest, space, samp, b, bit) for b in left]
                got_rest = swap(rest, "samp", samp, bit)
                near = [swap(rest, "space", space, b) for b in left]
                got = [got_own]
                for d in range(1, samp):
                    value = got_rest[d - 1]
                    for f in far:
                        value = value + f[d - 1]
                    got.append(value)
                for n in near:
                    done = [done[0]] + [done[d] + n[d - 1] for d in range(1, samp)]
            else:
                got = swap(jnp.stack(done), "samp", samp, bit)
            done = [done[d] + got[d ^ bit] for d in range(samp)]
        return jnp.stack(done)

    def shards(snapshots, space_basis, sample_basis):
        snaps, samples, columns = snapshots.shape
        rank = sample_basis.shape[1]
        basis_rows = space_basis.shape[0]
        wide = snaps * rank
        tile = tile_of(columns)
        steps = columns // tile
        others = [swap(space_basis, "samp", samp, d) for d in range(1, samp)]
        mixer = sample_basis.T
        flops = 6 * wide * samples * columns
        x_chip, mixed, own_split, own, spreader = pl.pallas_call(
            functools.partial(first_kernel, tile),
            out_shape=(
                on_chip(snapshots.shape, jnp.float32),
                on_chip((2, wide, columns), jnp.bfloat16),
                on_chip((2, basis_rows, columns), jnp.bfloat16),
                on_chip((wide, basis_rows), jnp.float32),
                on_chip((samples, 3 * rank), jnp.bfloat16),
            ),
            in_specs=[HBM, VMEM, HBM],
            out_specs=(VMEM,) * 5,
            scratch_shapes=[
                pltpu.VMEM((basis_rows, columns), jnp.float32),
                pltpu.SemaphoreType.DMA((steps,)),
                pltpu.SemaphoreType.DMA,
            ],
            compiler_params=pltpu.CompilerParams(vmem_limit_bytes=48 * MIB),
            cost_estimate=pl.CostEstimate(flops=flops, bytes_accessed=snapshots.size * 4, transcendentals=0),
            name="first",
        )(snapshots, mixer, space_basis)
        own = over_groups(halved(own))
        for bit in left:
            own = own + swap(own, "space", space, bit)
        rest, *rest_splits = pl.pallas_call(
            functools.partial(second_kernel, tile, samp - 1),
            out_shape=(
                on_chip((samp - 1, wide, basis_rows), jnp.float32),
                *[on_chip((2, basis_rows, columns), jnp.bfloat16) for _ in others],
            ),
            in_specs=[VMEM] * (len(others) + 1) + [ANY],
            out_specs=(VMEM,) * samp,
            compiler_params=pltpu.CompilerParams(vmem_limit_bytes=16 * MIB),
            cost_estimate=pl.CostEstimate(
                flops=6 * wide * basis_rows * columns * (samp - 1), bytes_accessed=0, transcendentals=0),
            name="second",
        )(*others, mixed, own)
        core = over_rest(own, over_groups(halved(rest)))
        other = swap(core, "space", space, 1)

        def last(mine, part, *out):
            fine = tile_of(columns, 256)
            return pl.pallas_call(
                functools.partial(last_kernel, fine, samp, mine),
                out_shape=jax.ShapeDtypeStruct(snapshots.shape, jnp.float32),
                in_specs=[VMEM] * (3 + samp) + [ANY] * len(out),
                out_specs=ANY,
                input_output_aliases={3 + samp: 0} if out else {},
                scratch_shapes=[
                    pltpu.VMEM((snaps // 2, samples, columns), jnp.float32),
                    pltpu.VMEM((2, wide // 2, columns), jnp.bfloat16),
                    pltpu.SemaphoreType.DMA((columns // fine,)),
                ],
                compiler_params=pltpu.CompilerParams(vmem_limit_bytes=20 * MIB),
                cost_estimate=pl.CostEstimate(flops=flops, bytes_accessed=snapshots.size * 2, transcendentals=0),
                name="last_mine" if mine else "last_other",
            )(part, spreader, x_chip, own_split, *rest_splits, *out)

        return last(False, other, last(True, core))

    return jax.shard_map(
        shards,
        mesh=mesh,
        in_specs=(P(None, "samp", "space"), P("samp", "space"), P("samp", None)),
        out_specs=P(None, "samp", "space"),
        check_vma=False,
    )
```

```python
import functools

import jax
import jax.numpy as jnp
from jax import lax
from jax.experimental import pallas as pl
from jax.experimental.pallas import tpu as pltpu
from jax.sharding import PartitionSpec as P


MIB = 1 << 20
AHEAD = 2


def swap(value, axis, size, bit):
    return lax.ppermute(value, axis, [(i, i ^ bit) for i in range(size)])


def bits(size, start=1):
    while start < size:
        yield start
        start *= 2


def swap_both(value, space, samp, bit, other):
    perm = [(i * samp + j, (i ^ bit) * samp + (j ^ other)) for i in range(space) for j in range(samp)]
    return lax.ppermute(value, ("space", "samp"), perm)


def tile_of(columns, most=512):
    for tile in (512, 256, 128):
        if tile <= most and columns % tile == 0:
            return tile
    return columns


def split(value):
    high = value.astype(jnp.bfloat16)
    return high, (value - high.astype(jnp.float32)).astype(jnp.bfloat16)


def mul(a, b):
    return lax.dot_general(a, b, (((1,), (0,)), ((), ())), preferred_element_type=jnp.float32)


def mul_t(a, b):
    return lax.dot_general(a, b, (((1,), (1,)), ((), ())), preferred_element_type=jnp.float32)


def rows_times(y_high, y_low, b):
    rank = b.shape[0]
    high, low = split(b)
    both = mul_t(y_high, jnp.concatenate([high, low], axis=0))
    return both[:, :rank] + both[:, rank:] + mul_t(y_low, high), high, low


def first_kernel(tile, x_hbm, s_ref, b_hbm, x_ref, y_ref, bs_ref, part_ref, spread_ref, b_ref, sems, b_sem):
    snaps, _, columns = x_ref.shape
    rank = s_ref.shape[0]
    steps = columns // tile
    copies = []
    for j in range(steps):
        cols = pl.ds(j * tile, tile)
        copies.append(pltpu.make_async_copy(x_hbm.at[:, :, cols], x_ref.at[:, :, cols], sems.at[j]))
    b_copy = pltpu.make_async_copy(b_hbm, b_ref, b_sem)
    copies[0].start()
    b_copy.start()
    for copy in copies[1:AHEAD]:
        copy.start()
    s_high, s_low = split(s_ref[...])
    s_both = jnp.concatenate([s_high, s_low], axis=0)
    t_high, t_low = split(s_ref[...].T)
    spread_ref[...] = jnp.concatenate([t_high, t_low, t_high], axis=1)
    for j in range(steps):
        cols = pl.ds(j * tile, tile)
        copies[j].wait()
        if j == 0:
            b_copy.wait()
        if j + AHEAD < steps:
            copies[j + AHEAD].start()
        for t in range(snaps):
            x_high, x_low = split(x_ref[t, :, cols])
            both = mul(s_both, x_high)
            y = both[:rank] + both[rank:] + mul(s_high, x_low)
            y_high, y_low = split(y)
            y_ref[0, t * rank:(t + 1) * rank, cols] = y_high
            y_ref[1, t * rank:(t + 1) * rank, cols] = y_low
        total, high, low = rows_times(y_ref[0, :, cols], y_ref[1, :, cols], b_ref[:, cols])
        bs_ref[0, :, cols] = high
        bs_ref[1, :, cols] = low
        if j == 0:
            part_ref[...] = total
        else:
            part_ref[...] += total


def second_kernel(tile, parts, *refs):
    b_refs, (y_ref, _), outs = refs[:parts], refs[parts:parts + 2], refs[parts + 2:]
    part_ref, bs_refs = outs[0], outs[1:]
    for d in range(parts):
        for j in range(y_ref.shape[2] // tile):
            cols = pl.ds(j * tile, tile)
            total, high, low = rows_times(y_ref[0, :, cols], y_ref[1, :, cols], b_refs[d][:, cols])
            bs_refs[d][0, :, cols] = high
            bs_refs[d][1, :, cols] = low
            if j == 0:
                part_ref[d] = total
            else:
                part_ref[d] += total


def last_kernel(tile, kept, parts, mine, *refs):
    core_ref, s_ref, x_ref = refs[:3]
    bs_refs = refs[3:3 + parts]
    if mine:
        out_hbm, kept_ref, out_ref, w_ref, sems = refs[3 + parts:]
    else:
        kept_ref, _, out_hbm, out_ref, w_ref, sems, kept_sem = refs[3 + parts:]
    half, columns = x_ref.shape[0] // 2, x_ref.shape[2]
    rank = s_ref.shape[1] // 3
    core = lax.axis_index("space") % 2
    start = half * (core if mine else 1 - core)
    whole = columns - kept
    if not mine:
        kept_copy = pltpu.make_async_copy(
            kept_ref, out_hbm.at[pl.ds(half - start, half), :, pl.ds(whole, kept)], kept_sem)
        kept_copy.start()
    c_high, c_low = split(jnp.concatenate([core_ref[d] for d in range(parts)], axis=1))
    c_both = jnp.concatenate([c_high, c_low], axis=0)
    wide = c_high.shape[0]
    steps = columns // tile

    def weigh(j):
        cols = pl.ds(j * tile, tile)
        b_high = jnp.concatenate([b[0, :, cols] for b in bs_refs], axis=0)
        b_low = jnp.concatenate([b[1, :, cols] for b in bs_refs], axis=0)
        both = mul(c_both, b_high)
        w_ref[0, :, cols], w_ref[1, :, cols] = split(both[:wide] + both[wide:] + mul(c_high, b_low))

    copies = []
    weigh(0)
    for j in range(steps):
        if j + 1 < steps:
            weigh(j + 1)
        cols = pl.ds(j * tile, tile)
        keep = mine and j * tile >= whole
        for t in range(half):
            high, low = w_ref[0, t * rank:(t + 1) * rank, cols], w_ref[1, t * rank:(t + 1) * rank, cols]
            removed = mul(s_ref[...], jnp.concatenate([high, high, low], axis=0))
            value = x_ref[start + t, :, cols] - removed
            if keep:
                kept_ref[t, :, pl.ds(j * tile - whole, tile)] = value
            else:
                out_ref[t, :, cols] = value
        if not keep:
            copies.append(pltpu.make_async_copy(
                out_ref.at[:, :, cols], out_hbm.at[pl.ds(start, half), :, cols], sems.at[j]))
            copies[-1].start()
    for copy in copies:
        copy.wait()
    if not mine:
        kept_copy.wait()


VMEM = pl.BlockSpec(memory_space=pltpu.VMEM)
ANY = pl.BlockSpec(memory_space=pl.ANY)
HBM = pl.BlockSpec(memory_space=pltpu.HBM)


def on_chip(shape, dtype):
    return pltpu.VMEM(shape, dtype)


def solution(mesh):
    space, samp = mesh.shape["space"], mesh.shape["samp"]

    left = list(bits(space, 2))
    groups = []
    while len(left) > 1:
        groups.append((left[-1], left[-2] | left[-1], left[-2]))
        left = left[:-2]

    def halved(part):
        core = lax.axis_index("space") % 2
        half = part.shape[-2] // 2
        low, high = part[..., :half, :], part[..., half:, :]
        mine = jnp.where(core == 0, low, high)
        return mine + swap(jnp.where(core == 0, high, low), "space", space, 1)

    def over_groups(part):
        for group in groups:
            got = [swap(part, "space", space, bit) for bit in group]
            part = part + got[0] + got[1] + got[2]
        return part

    def over_rest(own, rest):
        done = [own] + [rest[d] for d in range(samp - 1)]
        for bit in bits(samp):
            if bit == 1:
                got_own = swap(own, "samp", samp, bit)
                far = [swap_both(rest, space, samp, b, bit) for b in left]
                got_rest = swap(rest, "samp", samp, bit)
                near = [swap(rest, "space", space, b) for b in left]
                got = [got_own]
                for d in range(1, samp):
                    value = got_rest[d - 1]
                    for f in far:
                        value = value + f[d - 1]
                    got.append(value)
                for n in near:
                    done = [done[0]] + [done[d] + n[d - 1] for d in range(1, samp)]
            else:
                got = swap(jnp.stack(done), "samp", samp, bit)
            done = [done[d] + got[d ^ bit] for d in range(samp)]
        return jnp.stack(done)

    def shards(snapshots, space_basis, sample_basis):
        snaps, samples, columns = snapshots.shape
        rank = sample_basis.shape[1]
        basis_rows = space_basis.shape[0]
        wide = snaps * rank
        tile = tile_of(columns)
        steps = columns // tile
        others = [swap(space_basis, "samp", samp, d) for d in range(1, samp)]
        mixer = sample_basis.T
        flops = 6 * wide * samples * columns
        x_chip, mixed, own_split, own, spreader = pl.pallas_call(
            functools.partial(first_kernel, tile),
            out_shape=(
                on_chip(snapshots.shape, jnp.float32),
                on_chip((2, wide, columns), jnp.bfloat16),
                on_chip((2, basis_rows, columns), jnp.bfloat16),
                on_chip((wide, basis_rows), jnp.float32),
                on_chip((samples, 3 * rank), jnp.bfloat16),
            ),
            in_specs=[HBM, VMEM, HBM],
            out_specs=(VMEM,) * 5,
            scratch_shapes=[
                pltpu.VMEM((basis_rows, columns), jnp.float32),
                pltpu.SemaphoreType.DMA((steps,)),
                pltpu.SemaphoreType.DMA,
            ],
            compiler_params=pltpu.CompilerParams(vmem_limit_bytes=48 * MIB),
            cost_estimate=pl.CostEstimate(flops=flops, bytes_accessed=snapshots.size * 4, transcendentals=0),
            name="first",
        )(snapshots, mixer, space_basis)
        own = over_groups(halved(own))
        for bit in left:
            own = own + swap(own, "space", space, bit)
        rest, *rest_splits = pl.pallas_call(
            functools.partial(second_kernel, tile, samp - 1),
            out_shape=(
                on_chip((samp - 1, wide, basis_rows), jnp.float32),
                *[on_chip((2, basis_rows, columns), jnp.bfloat16) for _ in others],
            ),
            in_specs=[VMEM] * (len(others) + 1) + [ANY],
            out_specs=(VMEM,) * samp,
            compiler_params=pltpu.CompilerParams(vmem_limit_bytes=16 * MIB),
            cost_estimate=pl.CostEstimate(
                flops=6 * wide * basis_rows * columns * (samp - 1), bytes_accessed=0, transcendentals=0),
            name="second",
        )(*others, mixed, own)
        core = over_rest(own, over_groups(halved(rest)))
        other = swap(core, "space", space, 1)

        fine = tile_of(columns, 256)
        kept = columns // fine * 3 // 8 * fine

        def last(mine, part, *before):
            out = jax.ShapeDtypeStruct(snapshots.shape, jnp.float32)
            out_columns = columns - kept if mine else columns
            scratch = [
                pltpu.VMEM((snaps // 2, samples, out_columns), jnp.float32),
                pltpu.VMEM((2, wide // 2, columns), jnp.bfloat16),
                pltpu.SemaphoreType.DMA((out_columns // fine,)),
            ]
            return pl.pallas_call(
                functools.partial(last_kernel, fine, kept, samp, mine),
                out_shape=(out, on_chip((snaps // 2, samples, kept), jnp.float32)) if mine else out,
                in_specs=[VMEM] * (3 + samp) + ([] if mine else [VMEM, ANY]),
                out_specs=(ANY, VMEM) if mine else ANY,
                input_output_aliases={} if mine else {4 + samp: 0},
                scratch_shapes=scratch if mine else scratch + [pltpu.SemaphoreType.DMA],
                compiler_params=pltpu.CompilerParams(vmem_limit_bytes=20 * MIB),
                cost_estimate=pl.CostEstimate(flops=flops, bytes_accessed=snapshots.size * 2, transcendentals=0),
                name="last_mine" if mine else "last_other",
            )(part, spreader, x_chip, own_split, *rest_splits, *before)

        written, on_hold = last(True, core)
        return last(False, other, on_hold, written)

    return jax.shard_map(
        shards,
        mesh=mesh,
        in_specs=(P(None, "samp", "space"), P("samp", "space"), P("samp", None)),
        out_specs=P(None, "samp", "space"),
        check_vma=False,
    )
```

```python
import functools

import jax
import jax.numpy as jnp
from jax import lax
from jax.experimental import pallas as pl
from jax.experimental.pallas import tpu as pltpu
from jax.sharding import PartitionSpec as P


MIB = 1 << 20
AHEAD = 2


def swap(value, axis, size, bit):
    return lax.ppermute(value, axis, [(i, i ^ bit) for i in range(size)])


def bits(size, start=1):
    while start < size:
        yield start
        start *= 2


def swap_both(value, space, samp, bit, other):
    perm = [(i * samp + j, (i ^ bit) * samp + (j ^ other)) for i in range(space) for j in range(samp)]
    return lax.ppermute(value, ("space", "samp"), perm)


def tile_of(columns, most=512):
    for tile in (512, 256, 128):
        if tile <= most and columns % tile == 0:
            return tile
    return columns


def split(value):
    high = value.astype(jnp.bfloat16)
    return high, (value - high.astype(jnp.float32)).astype(jnp.bfloat16)


def mul(a, b):
    return lax.dot_general(a, b, (((1,), (0,)), ((), ())), preferred_element_type=jnp.float32)


def mul_t(a, b):
    return lax.dot_general(a, b, (((1,), (1,)), ((), ())), preferred_element_type=jnp.float32)


def rows_times(y_high, y_low, b):
    rank = b.shape[0]
    high, low = split(b)
    both = mul_t(y_high, jnp.concatenate([high, low], axis=0))
    return both[:, :rank] + both[:, rank:] + mul_t(y_low, high), high, low


def first_kernel(tile, x_hbm, s_ref, b_hbm, x_ref, y_ref, bs_ref, part_ref, spread_ref, b_ref, sems, b_sem):
    snaps, _, columns = x_ref.shape
    rank = s_ref.shape[0]
    steps = columns // tile
    copies = []
    for j in range(steps):
        cols = pl.ds(j * tile, tile)
        copies.append(pltpu.make_async_copy(x_hbm.at[:, :, cols], x_ref.at[:, :, cols], sems.at[j]))
    b_copy = pltpu.make_async_copy(b_hbm, b_ref, b_sem)
    copies[0].start()
    b_copy.start()
    for copy in copies[1:AHEAD]:
        copy.start()
    s_high, s_low = split(s_ref[...])
    s_both = jnp.concatenate([s_high, s_low], axis=0)
    t_high, t_low = split(s_ref[...].T)
    spread_ref[...] = jnp.concatenate([t_high, t_low, t_high], axis=1)
    for j in range(steps):
        cols = pl.ds(j * tile, tile)
        copies[j].wait()
        if j == 0:
            b_copy.wait()
        if j + AHEAD < steps:
            copies[j + AHEAD].start()
        for t in range(snaps):
            x_high, x_low = split(x_ref[t, :, cols])
            both = mul(s_both, x_high)
            y = both[:rank] + both[rank:] + mul(s_high, x_low)
            y_high, y_low = split(y)
            y_ref[0, t * rank:(t + 1) * rank, cols] = y_high
            y_ref[1, t * rank:(t + 1) * rank, cols] = y_low
        total, high, low = rows_times(y_ref[0, :, cols], y_ref[1, :, cols], b_ref[:, cols])
        bs_ref[0, :, cols] = high
        bs_ref[1, :, cols] = low
        if j == 0:
            part_ref[...] = total
        else:
            part_ref[...] += total


def second_kernel(tile, parts, mine, *refs):
    b_refs, y_ref, outs = refs[:parts], refs[parts], refs[-1 - parts if mine else -1:]
    part_ref, bs_refs = outs[0], outs[1:]
    half = y_ref.shape[1] // 2
    core = lax.axis_index("space") % 2
    rows = pl.ds(pl.multiple_of(half * (core if mine else 1 - core), half), half)
    for d in range(parts):
        for j in range(y_ref.shape[2] // tile):
            cols = pl.ds(j * tile, tile)
            total, high, low = rows_times(y_ref[0, rows, cols], y_ref[1, rows, cols], b_refs[d][:, cols])
            if mine:
                bs_refs[d][0, :, cols] = high
                bs_refs[d][1, :, cols] = low
            if j == 0:
                part_ref[d] = total
            else:
                part_ref[d] += total


def last_kernel(tile, kept, parts, mine, *refs):
    core_ref, s_ref, x_ref = refs[:3]
    bs_refs = refs[3:3 + parts]
    if mine:
        out_hbm, kept_ref, out_ref, w_ref, sems = refs[3 + parts:]
    else:
        kept_ref, _, out_hbm, out_ref, w_ref, sems, kept_sem = refs[3 + parts:]
    half, columns = x_ref.shape[0] // 2, x_ref.shape[2]
    rank = s_ref.shape[1] // 3
    core = lax.axis_index("space") % 2
    start = half * (core if mine else 1 - core)
    whole = columns - kept
    if not mine:
        kept_copy = pltpu.make_async_copy(
            kept_ref, out_hbm.at[pl.ds(half - start, half), :, pl.ds(whole, kept)], kept_sem)
        kept_copy.start()
    c_high, c_low = split(jnp.concatenate([core_ref[d] for d in range(parts)], axis=1))
    c_both = jnp.concatenate([c_high, c_low], axis=0)
    wide = c_high.shape[0]
    steps = columns // tile

    def weigh(j):
        cols = pl.ds(j * tile, tile)
        b_high = jnp.concatenate([b[0, :, cols] for b in bs_refs], axis=0)
        b_low = jnp.concatenate([b[1, :, cols] for b in bs_refs], axis=0)
        both = mul(c_both, b_high)
        w_ref[0, :, cols], w_ref[1, :, cols] = split(both[:wide] + both[wide:] + mul(c_high, b_low))

    copies = []
    weigh(0)
    for j in range(steps):
        if j + 1 < steps:
            weigh(j + 1)
        cols = pl.ds(j * tile, tile)
        keep = mine and j * tile >= whole
        for t in range(half):
            high, low = w_ref[0, t * rank:(t + 1) * rank, cols], w_ref[1, t * rank:(t + 1) * rank, cols]
            removed = mul(s_ref[...], jnp.concatenate([high, high, low], axis=0))
            value = x_ref[start + t, :, cols] - removed
            if keep:
                kept_ref[t, :, pl.ds(j * tile - whole, tile)] = value
            else:
                out_ref[t, :, cols] = value
        if not keep:
            copies.append(pltpu.make_async_copy(
                out_ref.at[:, :, cols], out_hbm.at[pl.ds(start, half), :, cols], sems.at[j]))
            copies[-1].start()
    for copy in copies:
        copy.wait()
    if not mine:
        kept_copy.wait()


VMEM = pl.BlockSpec(memory_space=pltpu.VMEM)
ANY = pl.BlockSpec(memory_space=pl.ANY)
HBM = pl.BlockSpec(memory_space=pltpu.HBM)


def on_chip(shape, dtype):
    return pltpu.VMEM(shape, dtype)


def solution(mesh):
    space, samp = mesh.shape["space"], mesh.shape["samp"]

    left = list(bits(space, 2))
    groups = []
    while len(left) > 1:
        groups.append((left[0] | left[1], left[1], left[0]))
        left = left[2:]

    def halved(part):
        core = lax.axis_index("space") % 2
        half = part.shape[-2] // 2
        low, high = part[..., :half, :], part[..., half:, :]
        mine = jnp.where(core == 0, low, high)
        return mine + swap(jnp.where(core == 0, high, low), "space", space, 1)

    def over_groups(part):
        for group in groups:
            got = [swap(part, "space", space, bit) for bit in group]
            part = part + got[0] + got[1] + got[2]
        return part

    def over_rest(own, rest):
        done = [own] + [rest[d] for d in range(samp - 1)]
        for bit in bits(samp):
            if bit == 1:
                got_own = swap(own, "samp", samp, bit)
                far = [swap_both(rest, space, samp, b, bit) for b in left]
                got_rest = swap(rest, "samp", samp, bit)
                near = [swap(rest, "space", space, b) for b in left]
                got = [got_own]
                for d in range(1, samp):
                    value = got_rest[d - 1]
                    for f in far:
                        value = value + f[d - 1]
                    got.append(value)
                for n in near:
                    done = [done[0]] + [done[d] + n[d - 1] for d in range(1, samp)]
            else:
                got = swap(jnp.stack(done), "samp", samp, bit)
            done = [done[d] + got[d ^ bit] for d in range(samp)]
        return jnp.stack(done)

    def shards(snapshots, space_basis, sample_basis):
        snaps, samples, columns = snapshots.shape
        rank = sample_basis.shape[1]
        basis_rows = space_basis.shape[0]
        wide = snaps * rank
        tile = tile_of(columns)
        steps = columns // tile
        others = [swap(space_basis, "samp", samp, d) for d in range(1, samp)]
        mixer = sample_basis.T
        flops = 6 * wide * samples * columns
        x_chip, mixed, own_split, own, spreader = pl.pallas_call(
            functools.partial(first_kernel, tile),
            out_shape=(
                on_chip(snapshots.shape, jnp.float32),
                on_chip((2, wide, columns), jnp.bfloat16),
                on_chip((2, basis_rows, columns), jnp.bfloat16),
                on_chip((wide, basis_rows), jnp.float32),
                on_chip((samples, 3 * rank), jnp.bfloat16),
            ),
            in_specs=[HBM, VMEM, HBM],
            out_specs=(VMEM,) * 5,
            scratch_shapes=[
                pltpu.VMEM((basis_rows, columns), jnp.float32),
                pltpu.SemaphoreType.DMA((steps,)),
                pltpu.SemaphoreType.DMA,
            ],
            compiler_params=pltpu.CompilerParams(vmem_limit_bytes=48 * MIB),
            cost_estimate=pl.CostEstimate(flops=flops, bytes_accessed=snapshots.size * 4, transcendentals=0),
            name="first",
        )(snapshots, mixer, space_basis)
        own = over_groups(halved(own))
        for bit in left:
            own = own + swap(own, "space", space, bit)

        def products(mine, after):
            return pl.pallas_call(
                functools.partial(second_kernel, tile, samp - 1, mine),
                out_shape=(
                    on_chip((samp - 1, wide // 2, basis_rows), jnp.float32),
                    *[on_chip((2, basis_rows, columns), jnp.bfloat16) for _ in others if mine],
                ),
                in_specs=[VMEM] * (len(others) + 1) + [ANY],
                out_specs=(VMEM,) * (samp if mine else 1),
                compiler_params=pltpu.CompilerParams(vmem_limit_bytes=16 * MIB),
                cost_estimate=pl.CostEstimate(
                    flops=3 * wide * basis_rows * columns * (samp - 1), bytes_accessed=0, transcendentals=0),
                name="second_mine" if mine else "second_other",
            )(*others, mixed, after)

        sent, = products(False, own)
        got = swap(sent, "space", space, 1)
        rest, *rest_splits = products(True, own)
        rest = rest + got
        core = over_rest(own, over_groups(rest))
        other = swap(core, "space", space, 1)

        fine = tile_of(columns, 256)
        kept = columns // fine * 3 // 8 * fine

        def last(mine, part, *before):
            out = jax.ShapeDtypeStruct(snapshots.shape, jnp.float32)
            out_columns = columns - kept if mine else columns
            scratch = [
                pltpu.VMEM((snaps // 2, samples, out_columns), jnp.float32),
                pltpu.VMEM((2, wide // 2, columns), jnp.bfloat16),
                pltpu.SemaphoreType.DMA((out_columns // fine,)),
            ]
            return pl.pallas_call(
                functools.partial(last_kernel, fine, kept, samp, mine),
                out_shape=(out, on_chip((snaps // 2, samples, kept), jnp.float32)) if mine else out,
                in_specs=[VMEM] * (3 + samp) + ([] if mine else [VMEM, ANY]),
                out_specs=(ANY, VMEM) if mine else ANY,
                input_output_aliases={} if mine else {4 + samp: 0},
                scratch_shapes=scratch if mine else scratch + [pltpu.SemaphoreType.DMA],
                compiler_params=pltpu.CompilerParams(vmem_limit_bytes=20 * MIB),
                cost_estimate=pl.CostEstimate(flops=flops, bytes_accessed=snapshots.size * 2, transcendentals=0),
                name="last_mine" if mine else "last_other",
            )(part, spreader, x_chip, own_split, *rest_splits, *before)

        written, on_hold = last(True, core)
        return last(False, other, on_hold, written)

    return jax.shard_map(
        shards,
        mesh=mesh,
        in_specs=(P(None, "samp", "space"), P("samp", "space"), P("samp", None)),
        out_specs=P(None, "samp", "space"),
        check_vma=False,
    )
```

```python
import functools

import jax
import jax.numpy as jnp
from jax import lax
from jax.experimental import pallas as pl
from jax.experimental.pallas import tpu as pltpu
from jax.sharding import PartitionSpec as P


MIB = 1 << 20
AHEAD = 2


def swap(value, axis, size, bit):
    return lax.ppermute(value, axis, [(i, i ^ bit) for i in range(size)])


def bits(size, start=1):
    while start < size:
        yield start
        start *= 2


def swap_both(value, space, samp, bit, other):
    perm = [(i * samp + j, (i ^ bit) * samp + (j ^ other)) for i in range(space) for j in range(samp)]
    return lax.ppermute(value, ("space", "samp"), perm)


def tile_of(columns, most=512):
    for tile in (512, 256, 128):
        if tile <= most and columns % tile == 0:
            return tile
    return columns


def split(value):
    high = value.astype(jnp.bfloat16)
    return high, (value - high.astype(jnp.float32)).astype(jnp.bfloat16)


def mul(a, b):
    return lax.dot_general(a, b, (((1,), (0,)), ((), ())), preferred_element_type=jnp.float32)


def mul_t(a, b):
    return lax.dot_general(a, b, (((1,), (1,)), ((), ())), preferred_element_type=jnp.float32)


def rows_times(y_high, y_low, b):
    rank = b.shape[0]
    high, low = split(b)
    both = mul_t(y_high, jnp.concatenate([high, low], axis=0))
    return both[:, :rank] + both[:, rank:] + mul_t(y_low, high), high, low


def first_kernel(tile, x_hbm, s_ref, b_hbm, x_ref, y_ref, bs_ref, part_ref, spread_ref, b_ref, sems, b_sem):
    snaps, _, columns = x_ref.shape
    rank = s_ref.shape[0]
    steps = columns // tile
    copies = []
    for j in range(steps):
        cols = pl.ds(j * tile, tile)
        copies.append(pltpu.make_async_copy(x_hbm.at[:, :, cols], x_ref.at[:, :, cols], sems.at[j]))
    b_copy = pltpu.make_async_copy(b_hbm, b_ref, b_sem)
    copies[0].start()
    b_copy.start()
    for copy in copies[1:AHEAD]:
        copy.start()
    s_high, s_low = split(s_ref[...])
    s_both = jnp.concatenate([s_high, s_low], axis=0)
    t_high, t_low = split(s_ref[...].T)
    spread_ref[...] = jnp.concatenate([t_high, t_low, t_high], axis=1)
    for j in range(steps):
        cols = pl.ds(j * tile, tile)
        copies[j].wait()
        if j == 0:
            b_copy.wait()
        if j + AHEAD < steps:
            copies[j + AHEAD].start()
        for t in range(snaps):
            x_high, x_low = split(x_ref[t, :, cols])
            both = mul(s_both, x_high)
            y = both[:rank] + both[rank:] + mul(s_high, x_low)
            y_high, y_low = split(y)
            y_ref[0, t * rank:(t + 1) * rank, cols] = y_high
            y_ref[1, t * rank:(t + 1) * rank, cols] = y_low
        total, high, low = rows_times(y_ref[0, :, cols], y_ref[1, :, cols], b_ref[:, cols])
        bs_ref[0, :, cols] = high
        bs_ref[1, :, cols] = low
        if j == 0:
            part_ref[...] = total
        else:
            part_ref[...] += total


def second_kernel(tile, parts, mine, *refs):
    b_refs, y_ref, outs = refs[:parts], refs[parts], refs[-1 - parts if mine else -1:]
    part_ref, bs_refs = outs[0], outs[1:]
    half = y_ref.shape[1] // 2
    core = lax.axis_index("space") % 2
    rows = pl.ds(pl.multiple_of(half * (core if mine else 1 - core), half), half)
    for d in range(parts):
        for j in range(y_ref.shape[2] // tile):
            cols = pl.ds(j * tile, tile)
            total, high, low = rows_times(y_ref[0, rows, cols], y_ref[1, rows, cols], b_refs[d][:, cols])
            if mine:
                bs_refs[d][0, :, cols] = high
                bs_refs[d][1, :, cols] = low
            if j == 0:
                part_ref[d] = total
            else:
                part_ref[d] += total


def last_kernel(tile, kept, parts, mine, *refs):
    core_ref, s_ref, x_ref = refs[:3]
    bs_refs = refs[3:3 + parts]
    if mine:
        out_hbm, kept_ref, out_ref, w_ref, sems = refs[3 + parts:]
    else:
        kept_ref, _, out_hbm, out_ref, w_ref, sems, kept_sem = refs[3 + parts:]
    half, columns = x_ref.shape[0] // 2, x_ref.shape[2]
    rank = s_ref.shape[1] // 3
    core = lax.axis_index("space") % 2
    start = half * (core if mine else 1 - core)
    whole = columns - kept
    if not mine:
        kept_copy = pltpu.make_async_copy(
            kept_ref, out_hbm.at[pl.ds(half - start, half), :, pl.ds(whole, kept)], kept_sem)
        kept_copy.start()
    c_high, c_low = split(jnp.concatenate([core_ref[d] for d in range(parts)], axis=1))
    c_both = jnp.concatenate([c_high, c_low], axis=0)
    wide = c_high.shape[0]
    steps = columns // tile

    def weigh(j):
        if j % 2:
            return
        cols = pl.ds(j * tile, 2 * tile)
        b_high = jnp.concatenate([b[0, :, cols] for b in bs_refs], axis=0)
        b_low = jnp.concatenate([b[1, :, cols] for b in bs_refs], axis=0)
        both = mul(c_both, b_high)
        w_ref[0, :, cols], w_ref[1, :, cols] = split(both[:wide] + both[wide:] + mul(c_high, b_low))

    copies = []
    weigh(0)
    for j in range(steps):
        if j + 2 < steps:
            weigh(j + 2)
        cols = pl.ds(j * tile, tile)
        keep = mine and j * tile >= whole
        for t in range(half):
            high, low = w_ref[0, t * rank:(t + 1) * rank, cols], w_ref[1, t * rank:(t + 1) * rank, cols]
            removed = mul(s_ref[...], jnp.concatenate([high, high, low], axis=0))
            value = x_ref[start + t, :, cols] - removed
            if keep:
                kept_ref[t, :, pl.ds(j * tile - whole, tile)] = value
            else:
                out_ref[t, :, cols] = value
        if not keep:
            copies.append(pltpu.make_async_copy(
                out_ref.at[:, :, cols], out_hbm.at[pl.ds(start, half), :, cols], sems.at[j]))
            copies[-1].start()
    for copy in copies:
        copy.wait()
    if not mine:
        kept_copy.wait()


VMEM = pl.BlockSpec(memory_space=pltpu.VMEM)
ANY = pl.BlockSpec(memory_space=pl.ANY)
HBM = pl.BlockSpec(memory_space=pltpu.HBM)


def on_chip(shape, dtype):
    return pltpu.VMEM(shape, dtype)


def solution(mesh):
    space, samp = mesh.shape["space"], mesh.shape["samp"]

    left = list(bits(space, 2))
    groups = []
    while len(left) > 1:
        groups.append((left[0] | left[1], left[1], left[0]))
        left = left[2:]

    def halved(part):
        core = lax.axis_index("space") % 2
        half = part.shape[-2] // 2
        low, high = part[..., :half, :], part[..., half:, :]
        mine = jnp.where(core == 0, low, high)
        return mine + swap(jnp.where(core == 0, high, low), "space", space, 1)

    def over_groups(part):
        for group in groups:
            got = [swap(part, "space", space, bit) for bit in group]
            part = part + got[0] + got[1] + got[2]
        return part

    def over_rest(own, rest):
        done = [own] + [rest[d] for d in range(samp - 1)]
        for bit in bits(samp):
            if bit == 1:
                got_own = swap(own, "samp", samp, bit)
                far = [swap_both(rest, space, samp, b, bit) for b in left]
                got_rest = swap(rest, "samp", samp, bit)
                near = [swap(rest, "space", space, b) for b in left]
                got = [got_own]
                for d in range(1, samp):
                    value = got_rest[d - 1]
                    for f in far:
                        value = value + f[d - 1]
                    got.append(value)
                for n in near:
                    done = [done[0]] + [done[d] + n[d - 1] for d in range(1, samp)]
            else:
                got = swap(jnp.stack(done), "samp", samp, bit)
            done = [done[d] + got[d ^ bit] for d in range(samp)]
        return jnp.stack(done)

    def shards(snapshots, space_basis, sample_basis):
        snaps, samples, columns = snapshots.shape
        rank = sample_basis.shape[1]
        basis_rows = space_basis.shape[0]
        wide = snaps * rank
        tile = tile_of(columns)
        steps = columns // tile
        others = [swap(space_basis, "samp", samp, d) for d in range(1, samp)]
        mixer = sample_basis.T
        flops = 6 * wide * samples * columns
        x_chip, mixed, own_split, own, spreader = pl.pallas_call(
            functools.partial(first_kernel, tile),
            out_shape=(
                on_chip(snapshots.shape, jnp.float32),
                on_chip((2, wide, columns), jnp.bfloat16),
                on_chip((2, basis_rows, columns), jnp.bfloat16),
                on_chip((wide, basis_rows), jnp.float32),
                on_chip((samples, 3 * rank), jnp.bfloat16),
            ),
            in_specs=[HBM, VMEM, HBM],
            out_specs=(VMEM,) * 5,
            scratch_shapes=[
                pltpu.VMEM((basis_rows, columns), jnp.float32),
                pltpu.SemaphoreType.DMA((steps,)),
                pltpu.SemaphoreType.DMA,
            ],
            compiler_params=pltpu.CompilerParams(vmem_limit_bytes=48 * MIB),
            cost_estimate=pl.CostEstimate(flops=flops, bytes_accessed=snapshots.size * 4, transcendentals=0),
            name="first",
        )(snapshots, mixer, space_basis)
        own = over_groups(halved(own))
        for bit in left:
            own = own + swap(own, "space", space, bit)

        def products(mine, after):
            return pl.pallas_call(
                functools.partial(second_kernel, tile, samp - 1, mine),
                out_shape=(
                    on_chip((samp - 1, wide // 2, basis_rows), jnp.float32),
                    *[on_chip((2, basis_rows, columns), jnp.bfloat16) for _ in others if mine],
                ),
                in_specs=[VMEM] * (len(others) + 1) + [ANY],
                out_specs=(VMEM,) * (samp if mine else 1),
                compiler_params=pltpu.CompilerParams(vmem_limit_bytes=16 * MIB),
                cost_estimate=pl.CostEstimate(
                    flops=3 * wide * basis_rows * columns * (samp - 1), bytes_accessed=0, transcendentals=0),
                name="second_mine" if mine else "second_other",
            )(*others, mixed, after)

        sent, = products(False, own)
        got = swap(sent, "space", space, 1)
        rest, *rest_splits = products(True, own)
        rest = rest + got
        core = over_rest(own, over_groups(rest))
        other = swap(core, "space", space, 1)

        fine = tile_of(columns, 256)
        kept = columns - fine

        def last(mine, part, *before):
            out = jax.ShapeDtypeStruct(snapshots.shape, jnp.float32)
            out_columns = columns - kept if mine else columns
            scratch = [
                pltpu.VMEM((snaps // 2, samples, out_columns), jnp.float32),
                pltpu.VMEM((2, wide // 2, columns), jnp.bfloat16),
                pltpu.SemaphoreType.DMA((out_columns // fine,)),
            ]
            return pl.pallas_call(
                functools.partial(last_kernel, fine, kept, samp, mine),
                out_shape=(out, on_chip((snaps // 2, samples, kept), jnp.float32)) if mine else out,
                in_specs=[VMEM] * (3 + samp) + ([] if mine else [VMEM, ANY]),
                out_specs=(ANY, VMEM) if mine else ANY,
                input_output_aliases={} if mine else {4 + samp: 0},
                scratch_shapes=scratch if mine else scratch + [pltpu.SemaphoreType.DMA],
                compiler_params=pltpu.CompilerParams(vmem_limit_bytes=20 * MIB),
                cost_estimate=pl.CostEstimate(flops=flops, bytes_accessed=snapshots.size * 2, transcendentals=0),
                name="last_mine" if mine else "last_other",
            )(part, spreader, x_chip, own_split, *rest_splits, *before)

        written, on_hold = last(True, core)
        return last(False, other, on_hold, written)

    return jax.shard_map(
        shards,
        mesh=mesh,
        in_specs=(P(None, "samp", "space"), P("samp", "space"), P("samp", None)),
        out_specs=P(None, "samp", "space"),
        check_vma=False,
    )
```

```python
import functools

import jax
import jax.numpy as jnp
from jax import lax
from jax.experimental import pallas as pl
from jax.experimental.pallas import tpu as pltpu
from jax.sharding import PartitionSpec as P


MIB = 1 << 20
AHEAD = 2


def swap(value, axis, size, bit):
    return lax.ppermute(value, axis, [(i, i ^ bit) for i in range(size)])


def bits(size, start=1):
    while start < size:
        yield start
        start *= 2


def swap_both(value, space, samp, bit, other):
    perm = [(i * samp + j, (i ^ bit) * samp + (j ^ other)) for i in range(space) for j in range(samp)]
    return lax.ppermute(value, ("space", "samp"), perm)


def tile_of(columns, most=512):
    for tile in (512, 256, 128):
        if tile <= most and columns % tile == 0:
            return tile
    return columns


def split(value):
    high = value.astype(jnp.bfloat16)
    return high, (value - high.astype(jnp.float32)).astype(jnp.bfloat16)


def mul(a, b):
    return lax.dot_general(a, b, (((1,), (0,)), ((), ())), preferred_element_type=jnp.float32)


def mul_t(a, b):
    return lax.dot_general(a, b, (((1,), (1,)), ((), ())), preferred_element_type=jnp.float32)


def rows_times(y_high, y_low, b):
    rank = b.shape[0]
    high, low = split(b)
    both = mul_t(y_high, jnp.concatenate([high, low], axis=0))
    return both[:, :rank] + both[:, rank:] + mul_t(y_low, high), high, low


def first_kernel(tile, x_hbm, s_ref, b_hbm, x_ref, y_ref, bs_ref, part_ref, spread_ref, b_ref, sems, b_sem):
    snaps, _, columns = x_ref.shape
    rank = s_ref.shape[0]
    steps = columns // tile
    copies = []
    for j in range(steps):
        cols = pl.ds(j * tile, tile)
        copies.append(pltpu.make_async_copy(x_hbm.at[:, :, cols], x_ref.at[:, :, cols], sems.at[j]))
    b_copy = pltpu.make_async_copy(b_hbm, b_ref, b_sem)
    copies[0].start()
    b_copy.start()
    for copy in copies[1:AHEAD]:
        copy.start()
    s_high, s_low = split(s_ref[...])
    s_both = jnp.concatenate([s_high, s_low], axis=0)
    t_high, t_low = split(s_ref[...].T)
    spread_ref[...] = jnp.concatenate([t_high, t_low, t_high], axis=1)
    for j in range(steps):
        cols = pl.ds(j * tile, tile)
        copies[j].wait()
        if j == 0:
            b_copy.wait()
        if j + AHEAD < steps:
            copies[j + AHEAD].start()
        for t in range(snaps):
            x_high, x_low = split(x_ref[t, :, cols])
            both = mul(s_both, x_high)
            y = both[:rank] + both[rank:] + mul(s_high, x_low)
            y_high, y_low = split(y)
            y_ref[0, t * rank:(t + 1) * rank, cols] = y_high
            y_ref[1, t * rank:(t + 1) * rank, cols] = y_low
        total, high, low = rows_times(y_ref[0, :, cols], y_ref[1, :, cols], b_ref[:, cols])
        bs_ref[0, :, cols] = high
        bs_ref[1, :, cols] = low
        if j == 0:
            part_ref[...] = total
        else:
            part_ref[...] += total


def second_kernel(tile, parts, mine, *refs):
    b_refs, y_ref, outs = refs[:parts], refs[parts], refs[-1 - parts if mine else -1:]
    part_ref, bs_refs = outs[0], outs[1:]
    half = y_ref.shape[1] // 2
    core = lax.axis_index("space") % 2
    rows = pl.ds(pl.multiple_of(half * (core if mine else 1 - core), half), half)
    for d in range(parts):
        rank = b_refs[d].shape[0]
        for j in range(y_ref.shape[2] // tile):
            cols = pl.ds(j * tile, tile)
            high, low = split(b_refs[d][:, cols])
            if mine:
                bs_refs[d][0, :, cols] = high
                bs_refs[d][1, :, cols] = low
            both = mul_t(y_ref[0, rows, cols], jnp.concatenate([high, low], axis=0))
            cross = mul_t(y_ref[1, rows, cols], high)
            both_sum = both if j == 0 else both_sum + both
            cross_sum = cross if j == 0 else cross_sum + cross
        part_ref[d] = both_sum[:, :rank] + both_sum[:, rank:] + cross_sum


def last_kernel(tile, kept, parts, mine, *refs):
    core_ref, s_ref, x_ref = refs[:3]
    bs_refs = refs[3:3 + parts]
    if mine:
        out_hbm, kept_ref, out_ref, w_ref, sems = refs[3 + parts:]
    else:
        kept_ref, _, out_hbm, out_ref, w_ref, sems, kept_sem = refs[3 + parts:]
    half, columns = x_ref.shape[0] // 2, x_ref.shape[2]
    rank = s_ref.shape[1] // 3
    core = lax.axis_index("space") % 2
    start = half * (core if mine else 1 - core)
    whole = columns - kept
    if not mine:
        kept_copy = pltpu.make_async_copy(
            kept_ref, out_hbm.at[pl.ds(half - start, half), :, pl.ds(whole, kept)], kept_sem)
        kept_copy.start()
    c_high, c_low = split(jnp.concatenate([core_ref[d] for d in range(parts)], axis=1))
    c_both = jnp.concatenate([c_high, c_low], axis=0)
    wide = c_high.shape[0]
    steps = columns // tile

    def weigh(j):
        if j % 2:
            return
        cols = pl.ds(j * tile, 2 * tile)
        b_high = jnp.concatenate([b[0, :, cols] for b in bs_refs], axis=0)
        b_low = jnp.concatenate([b[1, :, cols] for b in bs_refs], axis=0)
        both = mul(c_both, b_high)
        w_ref[0, :, cols], w_ref[1, :, cols] = split(both[:wide] + both[wide:] + mul(c_high, b_low))

    copies = []
    weigh(0)
    for j in range(steps):
        if j + 2 < steps:
            weigh(j + 2)
        cols = pl.ds(j * tile, tile)
        keep = mine and j * tile >= whole
        for t in range(half):
            high, low = w_ref[0, t * rank:(t + 1) * rank, cols], w_ref[1, t * rank:(t + 1) * rank, cols]
            removed = mul(s_ref[...], jnp.concatenate([high, high, low], axis=0))
            value = x_ref[start + t, :, cols] - removed
            if keep:
                kept_ref[t, :, pl.ds(j * tile - whole, tile)] = value
            else:
                out_ref[t, :, cols] = value
        if not keep:
            copies.append(pltpu.make_async_copy(
                out_ref.at[:, :, cols], out_hbm.at[pl.ds(start, half), :, cols], sems.at[j]))
            copies[-1].start()
    for copy in copies:
        copy.wait()
    if not mine:
        kept_copy.wait()


VMEM = pl.BlockSpec(memory_space=pltpu.VMEM)
ANY = pl.BlockSpec(memory_space=pl.ANY)
HBM = pl.BlockSpec(memory_space=pltpu.HBM)


def on_chip(shape, dtype):
    return pltpu.VMEM(shape, dtype)


def solution(mesh):
    space, samp = mesh.shape["space"], mesh.shape["samp"]

    left = list(bits(space, 2))
    groups = []
    while len(left) > 1:
        groups.append((left[0] | left[1], left[1], left[0]))
        left = left[2:]

    def halved(part):
        core = lax.axis_index("space") % 2
        half = part.shape[-2] // 2
        low, high = part[..., :half, :], part[..., half:, :]
        mine = jnp.where(core == 0, low, high)
        return mine + swap(jnp.where(core == 0, high, low), "space", space, 1)

    def over_groups(part):
        for group in groups:
            got = [swap(part, "space", space, bit) for bit in group]
            part = part + got[0] + got[1] + got[2]
        return part

    def over_rest(own, rest):
        done = [own] + [rest[d] for d in range(samp - 1)]
        for bit in bits(samp):
            if bit == 1:
                got_own = swap(own, "samp", samp, bit)
                far = [swap_both(rest, space, samp, b, bit) for b in left]
                got_rest = swap(rest, "samp", samp, bit)
                near = [swap(rest, "space", space, b) for b in left]
                got = [got_own]
                for d in range(1, samp):
                    value = got_rest[d - 1]
                    for f in far:
                        value = value + f[d - 1]
                    got.append(value)
                for n in near:
                    done = [done[0]] + [done[d] + n[d - 1] for d in range(1, samp)]
            else:
                got = swap(jnp.stack(done), "samp", samp, bit)
            done = [done[d] + got[d ^ bit] for d in range(samp)]
        return jnp.stack(done)

    def shards(snapshots, space_basis, sample_basis):
        snaps, samples, columns = snapshots.shape
        rank = sample_basis.shape[1]
        basis_rows = space_basis.shape[0]
        wide = snaps * rank
        tile = tile_of(columns)
        steps = columns // tile
        others = [swap(space_basis, "samp", samp, d) for d in range(1, samp)]
        mixer = sample_basis.T
        flops = 6 * wide * samples * columns
        x_chip, mixed, own_split, own, spreader = pl.pallas_call(
            functools.partial(first_kernel, tile),
            out_shape=(
                on_chip(snapshots.shape, jnp.float32),
                on_chip((2, wide, columns), jnp.bfloat16),
                on_chip((2, basis_rows, columns), jnp.bfloat16),
                on_chip((wide, basis_rows), jnp.float32),
                on_chip((samples, 3 * rank), jnp.bfloat16),
            ),
            in_specs=[HBM, VMEM, HBM],
            out_specs=(VMEM,) * 5,
            scratch_shapes=[
                pltpu.VMEM((basis_rows, columns), jnp.float32),
                pltpu.SemaphoreType.DMA((steps,)),
                pltpu.SemaphoreType.DMA,
            ],
            compiler_params=pltpu.CompilerParams(vmem_limit_bytes=48 * MIB),
            cost_estimate=pl.CostEstimate(flops=flops, bytes_accessed=snapshots.size * 4, transcendentals=0),
            name="first",
        )(snapshots, mixer, space_basis)
        own = over_groups(halved(own))
        for bit in left:
            own = own + swap(own, "space", space, bit)

        def products(mine, after):
            return pl.pallas_call(
                functools.partial(second_kernel, tile_of(columns, 256), samp - 1, mine),
                out_shape=(
                    on_chip((samp - 1, wide // 2, basis_rows), jnp.float32),
                    *[on_chip((2, basis_rows, columns), jnp.bfloat16) for _ in others if mine],
                ),
                in_specs=[VMEM] * (len(others) + 1) + [ANY],
                out_specs=(VMEM,) * (samp if mine else 1),
                compiler_params=pltpu.CompilerParams(vmem_limit_bytes=16 * MIB),
                cost_estimate=pl.CostEstimate(
                    flops=3 * wide * basis_rows * columns * (samp - 1), bytes_accessed=0, transcendentals=0),
                name="second_mine" if mine else "second_other",
            )(*others, mixed, after)

        sent, = products(False, own)
        got = swap(sent, "space", space, 1)
        rest, *rest_splits = products(True, own)
        rest = rest + got
        core = over_rest(own, over_groups(rest))
        other = swap(core, "space", space, 1)

        fine = tile_of(columns, 256)
        kept = columns - fine

        def last(mine, part, *before):
            out = jax.ShapeDtypeStruct(snapshots.shape, jnp.float32)
            out_columns = columns - kept if mine else columns
            scratch = [
                pltpu.VMEM((snaps // 2, samples, out_columns), jnp.float32),
                pltpu.VMEM((2, wide // 2, columns), jnp.bfloat16),
                pltpu.SemaphoreType.DMA((out_columns // fine,)),
            ]
            return pl.pallas_call(
                functools.partial(last_kernel, fine, kept, samp, mine),
                out_shape=(out, on_chip((snaps // 2, samples, kept), jnp.float32)) if mine else out,
                in_specs=[VMEM] * (3 + samp) + ([] if mine else [VMEM, ANY]),
                out_specs=(ANY, VMEM) if mine else ANY,
                input_output_aliases={} if mine else {4 + samp: 0},
                scratch_shapes=scratch if mine else scratch + [pltpu.SemaphoreType.DMA],
                compiler_params=pltpu.CompilerParams(vmem_limit_bytes=20 * MIB),
                cost_estimate=pl.CostEstimate(flops=flops, bytes_accessed=snapshots.size * 2, transcendentals=0),
                name="last_mine" if mine else "last_other",
            )(part, spreader, x_chip, own_split, *rest_splits, *before)

        written, on_hold = last(True, core)
        return last(False, other, on_hold, written)

    return jax.shard_map(
        shards,
        mesh=mesh,
        in_specs=(P(None, "samp", "space"), P("samp", "space"), P("samp", None)),
        out_specs=P(None, "samp", "space"),
        check_vma=False,
    )
```
